32 devices in a mesh: lat: 4 (over x, core), lon: 8 (over z, y).
Axes of the slice: x: 2, y: 2, z: 4, core: 2. Of those that a mesh axis runs over, the one named last changes fastest.
Arguments:
- start_state: float32 [256, 64, 1024], P('lat', None, 'lon'), may hold values from -6 to 6
- coefficients: float32 [5, 64], replicated, may hold values from 0.05 to 0.35
- w_in: bfloat16 [64, 512], replicated, may hold values from -0.75 to 0.75
- w_out: bfloat16 [512, 64], replicated, may hold values from -0.25 to 0.25
- jacobian: float32 [128, 64], replicated, may hold values from -0.75 to 0.75
- sigma: float32 [128], replicated, may hold values from 0.5 to 2
- obs_values: float32 [8192, 128], P(('lat', 'lon')), may hold values from -6 to 6
- owner: int32 [8192, 1], P(('lat', 'lon')), may hold values from 0 to 31; in each aligned block of 256 rows (0 to 255, 256 to 511, ...) at most 16 rows name the same one
- stencil: int32 [8192, 4], P(('lat', 'lon')), may hold values from 0 to 8191
- counts: int32 [8192], P(('lat', 'lon')), may hold values from 1 to 128
Outputs:
- grad_state: float32 [256, 64, 1024], P('lat', None, 'lon')
- departures: float32 [8192, 128], P(('lat', 'lon'))
- grad_w_in: float32 [64, 512], replicated
- grad_w_out: float32 [512, 64], replicated
The draws below stay inside these ranges and needn't reach their ends.
Inputs may be any that keep to these rules, and one draw needn't show every extreme that they name: owner is the tile's index lat * 8 + lon. Among the rows of one device no tile is named by more than 16 rows, a bound that some block reaches. `stencil`: A cell index inside the owning tile is its row times 128 plus its column.
All inputs are finite; a program needn't handle non-finite values.
Results may differ from the reference program's by a relative error of at most 0.0018.
The reference program's roundings to bfloat16 on the way count: a program that leaves them out, or rounds other values in their place, can miss the bound.
Values sent between devices are 32-bit elements; how exact they have to be, the bound alone decides.
A program may use at most 128 MiB of HBM per device.

```python
import math
import jax
import jax.numpy as jnp
import numpy as np
from jax import lax

HID = 512
CH = 128
TLAT = 64
TLON = 128
FEAT = 64
CAP = 16
OBS_DEV = 256
OBS = 8192
NLAT = 256
NLON = 1024
N_LON = 8
DEVICES = 32


def touch_ends(values, rng, smallest, top_value):
    place = [jax.random.randint(jax.random.fold_in(rng, axis), (), 0, length) for axis, length in enumerate(values.shape)]
    main_axis = values.shape.index(max(values.shape))
    next_to = place[:main_axis] + [(place[main_axis] + 1) % values.shape[main_axis]] + place[main_axis + 1:]
    return values.at[tuple(place)].set(smallest).at[tuple(next_to)].set(top_value)


def steps_of(rng, extent, cuts, smallest, top_value):
    def one(dim, blocks):
        draws = jax.random.uniform(jax.random.fold_in(jax.random.fold_in(rng, 6), dim), (blocks,), jnp.float32, smallest / len(cuts), top_value / len(cuts))
        return jnp.repeat(jnp.exp(draws), extent[dim] // blocks).reshape((-1,) + (1,) * (len(extent) - dim - 1))

    loudness = one(*cuts[0])
    for cut in cuts[1:]:
        loudness = loudness * one(*cut)
    return loudness


def deal_out(key, own, number, rows, number_of, top, bound, skew):
    order = jax.random.permutation(key, number_of)
    crowded, common = load_shares(number_of, rows * top, bound, skew, True), load_shares(number_of, rows * top, bound, skew, False)
    places = jnp.arange(number_of)

    def named(tallies, offset_by):
        used = int((tallies > 0).sum())
        fixed = max(1, used // 4)
        moved = fixed + (places - fixed + offset_by * (used - fixed)) % max(1, number_of - fixed)
        return jnp.zeros((number_of,), jnp.int32).at[order[jnp.where(places < fixed, places, moved)]].set(jnp.asarray(tallies, jnp.int32))

    tallies = jnp.where(number % 4 == 0, named(crowded, number // 4), named(common, number - number // 4 - 1))
    mixed = jax.random.permutation(jax.random.fold_in(own, 3), number_of)
    source_of, sink = mixed[0:number_of // 2 * 2:2], mixed[1:number_of // 2 * 2:2]
    margin = jnp.minimum(tallies[source_of] - 1, bound - tallies[sink]) // 2
    margin = jnp.where((source_of == order[0]) | (sink == order[0]) | (tallies[sink] == 0), 0, jnp.maximum(margin, 0))
    moved = jax.random.randint(jax.random.fold_in(own, 4), (number_of // 2,), 0, 1 << 20) % (margin + 1)
    tallies = tallies.at[source_of].add(-moved).at[sink].add(moved)
    labels = jnp.searchsorted(jnp.cumsum(tallies), jnp.arange(rows * top), side="right").astype(jnp.int32)
    grid = labels.reshape(top, rows).T
    grid = grid[jax.random.permutation(jax.random.fold_in(own, 1), rows)]
    offset_by = jax.random.randint(jax.random.fold_in(own, 2), (rows, 1), 0, top)
    return jnp.take_along_axis(grid, (jnp.arange(top)[None, :] + offset_by) % top, axis=1)


def load_shares(count, total, reach, slope, full):
    weights = [(1 << 20) // math.isqrt(standing ** slope) + 1 for standing in range(1, count + 1)]
    largest = reach if full else min(reach, max(-(-total // count), total * weights[0] // sum(weights)))
    least = 1 if total - largest >= count - 1 else 0
    holding, spare = [largest] + [least] * (count - 1), total - largest - least * (count - 1)
    while spare > 0:
        candidates = [i for i in range(1, count) if holding[i] < largest] or [i for i in range(1, count) if holding[i] < reach]
        pool, budget = sum([weights[i] for i in candidates]), spare
        for i in candidates:
            addition = min(reach - holding[i], max(1, budget * weights[i] // pool), spare)
            holding[i] = holding[i] + addition
            spare = spare - addition
    return np.array(holding)


def noise(stream_key, dims, deviation, most, shards=(), kind=jnp.bfloat16):
    gain = steps_of(stream_key, dims, shards, -0.22, 0.18) if shards else 1.0
    entries = jax.random.normal(stream_key, dims, jnp.float32) * deviation * gain
    return jnp.minimum(jnp.maximum(entries, -most), most).astype(kind)


def setup_inputs(seed: int = 0) -> dict:
    arg_keys = jax.random.split(jax.random.key(seed), 11)
    start_state = noise(arg_keys[0], (NLAT, FEAT, NLON), 1.0, 6.0, ((0, 4), (2, 8)), jnp.float32)
    coefficients = jnp.clip(jax.random.uniform(arg_keys[1], (5, FEAT), jnp.float32, 0.05, 0.35), 0.05, 0.35)
    w_in = noise(arg_keys[2], (FEAT, HID), FEAT ** -0.5, 0.75)
    w_out = noise(arg_keys[3], (HID, FEAT), HID ** -0.5, 0.25)
    jacobian = noise(arg_keys[4], (CH, FEAT), FEAT ** -0.5, 0.75, (), jnp.float32)
    sigma = jnp.clip(jnp.exp(jax.random.uniform(arg_keys[5], (CH,), jnp.float32, math.log(0.5), math.log(2.0))), 0.5, 2.0)
    obs_values = noise(arg_keys[6], (OBS, CH), 1.0, 6.0, ((0, 32),), jnp.float32)
    owner_keys = jax.random.split(jax.random.fold_in(arg_keys[7], 1), OBS // OBS_DEV)
    owner_turns = jax.random.permutation(jax.random.fold_in(arg_keys[7], 3), OBS // OBS_DEV)
    owner = jax.vmap(lambda own, number: deal_out(jax.random.fold_in(arg_keys[7], 2), own, number, OBS_DEV, DEVICES, 1, CAP, 2))(owner_keys, owner_turns).reshape((OBS, 1))
    stencil = touch_ends(jax.random.randint(arg_keys[8], (OBS, 4), 0, TLAT * TLON), jax.random.fold_in(arg_keys[8], 1), 0, (TLAT * TLON) - 1).astype(jnp.int32)
    counts = touch_ends(jax.random.randint(arg_keys[9], (OBS,), 1, CH + 1), jax.random.fold_in(arg_keys[9], 1), 1, CH).astype(jnp.int32)
    return {"start_state": start_state, "coefficients": coefficients, "w_in": w_in, "w_out": w_out, "jacobian": jacobian, "sigma": sigma, "obs_values": obs_values, "owner": owner, "stencil": stencil, "counts": counts}


interp_weights = (0.4, 0.3, 0.2, 0.1)

def group_size(nrows, width, target):
    group = max(1, min(nrows, target // width))
    while nrows % group:
        group -= 1
    return group

def stencil_apply(state, coefficients):
    padded = jnp.pad(state, ((1, 1), (0, 0), (0, 0)))
    scaled = coefficients[:, None, :, None]
    west = jnp.roll(state, 1, axis=2)
    east = jnp.roll(state, -1, axis=2)
    return scaled[0] * state + scaled[1] * padded[:-2] + scaled[2] * padded[2:] + scaled[3] * west + scaled[4] * east

def stencil_adjoint(field, coefficients):
    padded = jnp.pad(field, ((1, 1), (0, 0), (0, 0)))
    scaled = coefficients[:, None, :, None]
    ahead = jnp.roll(field, -1, axis=2)
    behind = jnp.roll(field, 1, axis=2)
    return scaled[0] * field + scaled[1] * padded[2:] + scaled[2] * padded[:-2] + scaled[3] * ahead + scaled[4] * behind

def closure_block(block, w_in, w_out):
    inputs = block.astype(jnp.bfloat16).astype(jnp.float32)
    pre = jnp.einsum('fh,gfw->ghw', w_in.astype(jnp.float32), inputs)
    hidden = jnp.tanh(pre).astype(jnp.bfloat16).astype(jnp.float32)
    return jnp.einsum('hf,ghw->gfw', w_out.astype(jnp.float32), hidden)

def closure_forward(state, w_in, w_out):
    nrows, feat, width = state.shape
    group = group_size(nrows, width, 8192)
    blocks = state.reshape(nrows // group, group, feat, width)
    result = lax.map(lambda block: closure_block(block, w_in, w_out), blocks)
    return result.reshape(nrows, feat, width)

def closure_backward(state, cotangent, w_in, w_out):
    nrows, feat, width = state.shape
    group = group_size(nrows, width, 8192)
    blocks = state.reshape(nrows // group, group, feat, width)
    cot_blocks = cotangent.reshape(nrows // group, group, feat, width)
    w_in32 = w_in.astype(jnp.float32)
    w_out32 = w_out.astype(jnp.float32)

    def one_block(carry, pieces):
        block, cot_block = pieces
        inputs = block.astype(jnp.bfloat16).astype(jnp.float32)
        pre = jnp.einsum('fh,gfw->ghw', w_in32, inputs)
        tanh_pre = jnp.tanh(pre)
        hidden = tanh_pre.astype(jnp.bfloat16).astype(jnp.float32)
        cot_low = cot_block.astype(jnp.bfloat16).astype(jnp.float32)
        grad_out = jnp.einsum('ghw,gfw->hf', hidden, cot_low)
        back_hidden = jnp.einsum('hf,gfw->ghw', w_out32, cot_low)
        back_pre = (back_hidden * (1.0 - tanh_pre * tanh_pre)).astype(jnp.bfloat16).astype(jnp.float32)
        grad_in = jnp.einsum('gfw,ghw->fh', inputs, back_pre)
        back_state = jnp.einsum('fh,ghw->gfw', w_in32, back_pre)
        return ((carry[0] + grad_in, carry[1] + grad_out), back_state)
    init = (jnp.zeros((feat, w_in.shape[1]), jnp.float32), jnp.zeros((w_in.shape[1], feat), jnp.float32))
    totals, back = lax.scan(one_block, init, (blocks, cot_blocks))
    return (back.reshape(nrows, feat, width), totals[0], totals[1])

def reference(start_state, coefficients, w_in, w_out, jacobian, sigma, obs_values, owner, stencil, counts):
    state_one = stencil_apply(start_state, coefficients) + closure_forward(start_state, w_in, w_out)
    state_two = stencil_apply(state_one, coefficients) + closure_forward(state_one, w_in, w_out)
    tile_owner = owner[:, 0]
    row_base = tile_owner // N_LON * TLAT
    col_base = tile_owner % N_LON * TLON
    row_ids = (row_base[:, None] + stencil // TLON).astype(jnp.int32)
    col_ids = (col_base[:, None] + stencil % TLON).astype(jnp.int32)
    interp = interp_weights[0] * state_two[row_ids[:, 0], :, col_ids[:, 0]]
    for corner in range(1, 4):
        interp = interp + interp_weights[corner] * state_two[row_ids[:, corner], :, col_ids[:, corner]]
    evolved = jnp.dot(interp, jacobian.T, precision=lax.Precision.HIGHEST, preferred_element_type=jnp.float32)
    channel = jnp.arange(CH, dtype=jnp.int32)
    used = channel[None, :] < counts[:, None]
    departures = jnp.where(used, (obs_values - evolved) / sigma[None, :], 0.0)
    pulled = jnp.dot(-departures / sigma[None, :], jacobian, precision=lax.Precision.HIGHEST, preferred_element_type=jnp.float32)
    adjoint_two = jnp.zeros_like(state_two)
    for corner in range(4):
        adjoint_two = adjoint_two.at[row_ids[:, corner], :, col_ids[:, corner]].add(interp_weights[corner] * pulled)
    back_one, gin_one, gout_one = closure_backward(state_one, adjoint_two, w_in, w_out)
    adjoint_one = stencil_adjoint(adjoint_two, coefficients) + back_one
    back_zero, gin_zero, gout_zero = closure_backward(start_state, adjoint_one, w_in, w_out)
    grad_state = stencil_adjoint(adjoint_one, coefficients) + back_zero
    scale = 1.0 / math.sqrt(NLAT * NLON)
    return (grad_state, departures, (gin_one + gin_zero) * scale, (gout_one + gout_zero) * scale)
```

```python
import functools
import math

import jax
import jax.numpy as jnp
from jax import lax
from jax.experimental import pallas as pl
from jax.experimental.pallas import tpu as pltpu
from jax.sharding import PartitionSpec as P

CAP = 16
GROUP = 4
VMEM_LIMIT = 48 * 1024 * 1024
corner_tenths = (4, 3, 2, 1)
TENTH = 0.1


def fill_rows(rows, x_ref, north_ref, south_ref):
    count = x_ref.shape[0]
    rows[pl.ds(1, count)] = x_ref[...]
    rows[0] = north_ref[...]
    rows[count + 1] = south_ref[...]


def stencil_row(rows, left, right, weights, i):
    count, (feat, width) = rows.shape[0] - 2, rows.shape[1:]
    lane = lax.broadcasted_iota(jnp.int32, (feat, width), 1)
    here = rows[i + 1]
    west = jnp.where(
        lane == 0, pltpu.roll(left, width - count - i, axis=1), pltpu.roll(here, 1, axis=1)
    )
    east = jnp.where(
        lane == width - 1,
        pltpu.roll(right, width - 1 - i, axis=1),
        pltpu.roll(here, width - 1, axis=1),
    )
    return (
        weights[0] * here
        + weights[1] * rows[i]
        + weights[2] * rows[i + 2]
        + weights[3] * west
        + weights[4] * east
    )


def keep_edges(edge_ref, row, i, count):
    feat, width = row.shape
    lane = lax.broadcasted_iota(jnp.int32, (feat, width), 1)
    edge_ref[...] = jnp.where(
        lane == i,
        pltpu.roll(row, i, axis=1),
        jnp.where(
            lane == count + i,
            pltpu.roll(row, lax.rem(count + i + 1, width), axis=1),
            edge_ref[...],
        ),
    )


def weights_of(c_ref, order, width):
    feat = c_ref.shape[0]
    return [jnp.broadcast_to(c_ref[:, k : k + 1], (feat, width)) for k in order]


def mm(a, b):
    return jnp.dot(a, b, preferred_element_type=jnp.float32)


def mm_nt(a, b):
    return lax.dot_general(a, b, (((1,), (1,)), ((), ())), preferred_element_type=jnp.float32)


def two_parts(x):
    high = x.astype(jnp.bfloat16)
    low = (x - high.astype(jnp.float32)).astype(jnp.bfloat16)
    return jnp.concatenate([high, low], axis=0)


def forward_group(rows, left, right, weights, wit_ref, wot_ref, base):
    width = rows.shape[2]
    inputs = jnp.concatenate([rows[base + g + 1] for g in range(GROUP)], axis=1).astype(
        jnp.bfloat16
    )
    hidden = jnp.tanh(mm(wit_ref[...], inputs)).astype(jnp.bfloat16)
    closure = mm(wot_ref[...], hidden)
    return [
        stencil_row(rows, left, right, weights, base + g) + closure[:, g * width : (g + 1) * width]
        for g in range(GROUP)
    ]


def forward_kernel(
    x_ref, n_ref, s_ref, l_ref, r_ref, c_ref, wit_ref, wot_ref, o_ref, edge_ref, rows
):
    count, feat, width = x_ref.shape
    fill_rows(rows, x_ref, n_ref, s_ref)
    edge_ref[...] = jnp.zeros_like(edge_ref)

    def step(b, carry):
        base = b * GROUP
        weights = weights_of(c_ref, (0, 1, 2, 3, 4), width)
        out = forward_group(
            rows, l_ref[...], r_ref[...], weights, wit_ref, wot_ref, base
        )
        for g in range(GROUP):
            o_ref[base + g] = out[g]
            keep_edges(edge_ref, out[g], base + g, count)
        return carry

    lax.fori_loop(0, count // GROUP, step, 0)


def forward_interp_kernel(
    x_ref, n_ref, s_ref, l_ref, r_ref, c_ref, wit_ref, wot_ref, cell_ref, o_ref, rows, acc
):
    count, feat, width = x_ref.shape
    slots = cell_ref.shape[1]
    block = min(slots, 512)
    fill_rows(rows, x_ref, n_ref, s_ref)
    acc[...] = jnp.zeros_like(acc)

    def step(b, carry):
        base = b * GROUP
        weights = weights_of(c_ref, (0, 1, 2, 3, 4), width)
        out = forward_group(
            rows, l_ref[...], r_ref[...], weights, wit_ref, wot_ref, base
        )
        parts = two_parts(jnp.concatenate(out, axis=1))
        for s in range(0, slots, block):
            cell = (
                lax.broadcasted_iota(jnp.int32, (GROUP * width, block), 0) + base * width
            )
            pick = jnp.zeros((GROUP * width, block), jnp.float32)
            for k in range(4):
                pick = pick + jnp.where(
                    cell == cell_ref[k : k + 1, s : s + block], float(corner_tenths[k]), 0.0
                )
            both = mm(parts, pick.astype(jnp.bfloat16))
            acc[:, s : s + block] += both[:feat] + both[feat:]
        return carry

    lax.fori_loop(0, count // GROUP, step, 0)
    o_ref[...] = jnp.transpose(acc[...] * TENTH)


def spread_kernel(pulled_ref, cell_ref, o_ref, edge_ref, parts):
    count, feat, width = o_ref.shape
    slots = cell_ref.shape[0]
    edge_ref[...] = jnp.zeros_like(edge_ref)
    parts[...] = two_parts(jnp.transpose(pulled_ref[...]) * TENTH)
    block = min(slots, 512)

    def step(b, carry):
        base = b * GROUP
        total = jnp.zeros((2 * feat, GROUP * width), jnp.float32)
        for s in range(0, slots, block):
            cell = (
                lax.broadcasted_iota(jnp.int32, (block, GROUP * width), 1) + base * width
            )
            pick = jnp.zeros((block, GROUP * width), jnp.float32)
            for k in range(4):
                pick = pick + jnp.where(
                    cell == cell_ref[s : s + block, k : k + 1], float(corner_tenths[k]), 0.0
                )
            total = total + mm(parts[:, s : s + block], pick.astype(jnp.bfloat16))
        out = total[:feat] + total[feat:]
        for g in range(GROUP):
            row = out[:, g * width : (g + 1) * width]
            o_ref[base + g] = row
            keep_edges(edge_ref, row, base + g, count)
        return carry

    lax.fori_loop(0, count // GROUP, step, 0)


def backward_kernel(
    v_ref,
    x_ref,
    n_ref,
    s_ref,
    l_ref,
    r_ref,
    c_ref,
    wit_ref,
    wi_ref,
    wo_ref,
    o_ref,
    edge_ref,
    grad_ref,
    rows,
    gin,
    gout,
):
    count, feat, width = x_ref.shape
    fill_rows(rows, x_ref, n_ref, s_ref)
    edge_ref[...] = jnp.zeros_like(edge_ref)
    gin[...] = jnp.zeros_like(gin)
    gout[...] = jnp.zeros_like(gout)

    def step(b, carry):
        base = b * GROUP
        weights = weights_of(c_ref, (0, 2, 1, 4, 3), width)
        inputs = jnp.concatenate([v_ref[base + g] for g in range(GROUP)], axis=1).astype(
            jnp.bfloat16
        )
        cot = jnp.concatenate([rows[base + g + 1] for g in range(GROUP)], axis=1).astype(
            jnp.bfloat16
        )
        tanh_pre = jnp.tanh(mm(wit_ref[...], inputs))
        hidden = tanh_pre.astype(jnp.bfloat16)
        gout[...] += mm_nt(hidden, cot)
        back_hidden = mm(wo_ref[...], cot)
        back_pre = (back_hidden * (1.0 - tanh_pre * tanh_pre)).astype(jnp.bfloat16)
        gin[...] += mm_nt(back_pre, inputs)
        back = mm(wi_ref[...], back_pre)
        for g in range(GROUP):
            row = (
                stencil_row(rows, l_ref[...], r_ref[...], weights, base + g)
                + back[:, g * width : (g + 1) * width]
            )
            o_ref[base + g] = row
            keep_edges(edge_ref, row, base + g, count)
        return carry

    lax.fori_loop(0, count // GROUP, step, 0)
    grad_ref[...] = jnp.concatenate([gin[...], gout[...]], axis=1)


def call(kernel, outs, scratch, *args):
    return pl.pallas_call(
        kernel,
        out_shape=outs,
        in_specs=[pl.BlockSpec(memory_space=pltpu.VMEM)] * len(args),
        out_specs=jax.tree.map(lambda _: pl.BlockSpec(memory_space=pltpu.VMEM), outs),
        scratch_shapes=scratch,
        compiler_params=pltpu.CompilerParams(vmem_limit_bytes=VMEM_LIMIT),
    )(*args)


def halos(field, edges):
    lat, lon = lax.axis_size("lat"), lax.axis_size("lon")
    south = [(i, i + 1) for i in range(lat - 1)]
    north = [(i + 1, i) for i in range(lat - 1)]
    east = [(i, (i + 1) % lon) for i in range(lon)]
    west = [((i + 1) % lon, i) for i in range(lon)]
    return (
        lax.ppermute(field[-1], "lat", south),
        lax.ppermute(field[0], "lat", north),
        lax.ppermute(edges, "lon", east),
        lax.ppermute(edges, "lon", west),
    )


def swap(blocks):
    return lax.all_to_all(blocks, ("lat", "lon"), split_axis=0, concat_axis=0, tiled=True)


def f32(*shape):
    return jax.ShapeDtypeStruct(shape, jnp.float32)


def on_device(
    start_state, coefficients, w_in, w_out, jacobian, sigma, obs_values, owner, stencil, counts
):
    tlat, feat, tlon = start_state.shape
    hid = w_in.shape[1]
    lat_count = lax.axis_size("lat")
    lon_count = lax.axis_size("lon")
    devices = lat_count * lon_count
    channels = obs_values.shape[1]
    slots = devices * CAP
    rows_scratch = pltpu.VMEM((tlat + 2, feat, tlon), jnp.float32)
    tile, edge_shape = f32(tlat, feat, tlon), f32(feat, tlon)

    tile_owner = owner[:, 0]
    onehot = (tile_owner[:, None] == jnp.arange(devices, dtype=jnp.int32)[None, :]).astype(
        jnp.int32
    )
    running = jnp.cumsum(onehot, axis=0)
    rank = jnp.sum(running * onehot, axis=1) - 1
    slot = tile_owner * CAP + rank
    send_stencil = jnp.zeros((slots, 4), jnp.int32).at[slot].set(stencil)
    cell_recv = swap(send_stencil)

    coef = coefficients.T
    w_in_t, w_out_t = w_in.T, w_out.T
    start_edges = jnp.concatenate([start_state[:, :, 0].T, start_state[:, :, -1].T], axis=1)
    state_one, edges_one = call(
        forward_kernel,
        (tile, edge_shape),
        [rows_scratch],
        start_state,
        *halos(start_state, start_edges),
        coef,
        w_in_t,
        w_out_t,
    )
    slot_interp = call(
        forward_interp_kernel,
        f32(slots, feat),
        [rows_scratch, pltpu.VMEM((feat, slots), jnp.float32)],
        state_one,
        *halos(state_one, edges_one),
        coef,
        w_in_t,
        w_out_t,
        cell_recv.T,
    )
    row_interp = swap(slot_interp)[slot]
    evolved = jnp.dot(
        row_interp, jacobian.T, precision=lax.Precision.HIGHEST, preferred_element_type=jnp.float32
    )
    used = jnp.arange(channels, dtype=jnp.int32)[None, :] < counts[:, None]
    departures = jnp.where(used, (obs_values - evolved) / sigma[None, :], 0.0)
    row_pulled = jnp.dot(
        -departures / sigma[None, :],
        jacobian,
        precision=lax.Precision.HIGHEST,
        preferred_element_type=jnp.float32,
    )
    recv_pulled = swap(jnp.zeros((slots, feat), jnp.float32).at[slot].set(row_pulled))
    adjoint_two, edges_two = call(
        spread_kernel,
        (tile, edge_shape),
        [pltpu.VMEM((2 * feat, slots), jnp.bfloat16)],
        recv_pulled,
        cell_recv,
    )

    def backward(state, cotangent, edges):
        return call(
            backward_kernel,
            (tile, edge_shape, f32(hid, 2 * feat)),
            [rows_scratch] + [pltpu.VMEM((hid, feat), jnp.float32)] * 2,
            state,
            cotangent,
            *halos(cotangent, edges),
            coef,
            w_in_t,
            w_in,
            w_out,
        )

    adjoint_one, edges_adj, grads_one = backward(state_one, adjoint_two, edges_two)
    grad_state, _, grads_zero = backward(start_state, adjoint_one, edges_adj)
    grads = (grads_one + grads_zero).reshape(devices, hid // devices, 2 * feat)
    part = jnp.sum(swap(grads), axis=0)
    scale = 1.0 / math.sqrt(tlat * lat_count * tlon * lon_count)
    part = part * scale
    total = swap(jnp.broadcast_to(part[None], grads.shape)).reshape(hid, 2 * feat)
    return (grad_state, departures, total[:, :feat].T, total[:, feat:])


def solution(mesh):
    return jax.shard_map(
        on_device,
        mesh=mesh,
        in_specs=(
            P("lat", None, "lon"),
            P(),
            P(),
            P(),
            P(),
            P(),
            P(("lat", "lon"), None),
            P(("lat", "lon"), None),
            P(("lat", "lon"), None),
            P(("lat", "lon")),
        ),
        out_specs=(P("lat", None, "lon"), P(("lat", "lon"), None), P(), P()),
        check_vma=False,
    )
```

```python
import functools
import math

import jax
import jax.numpy as jnp
from jax import lax
from jax.experimental import pallas as pl
from jax.experimental.pallas import tpu as pltpu
from jax.sharding import PartitionSpec as P

CAP = 16
GROUP = 4
VMEM_LIMIT = 48 * 1024 * 1024
corner_tenths = (4, 3, 2, 1)
TENTH = 0.1


def fill_rows(rows, x_ref, north_ref, south_ref):
    count = x_ref.shape[0]
    rows[pl.ds(1, count)] = x_ref[...]
    rows[0] = north_ref[...]
    rows[count + 1] = south_ref[...]


def stencil_row(rows, left, right, weights, i):
    count, (feat, width) = rows.shape[0] - 2, rows.shape[1:]
    lane = lax.broadcasted_iota(jnp.int32, (feat, width), 1)
    here = rows[i + 1]
    west = jnp.where(
        lane == 0, pltpu.roll(left, width - count - i, axis=1), pltpu.roll(here, 1, axis=1)
    )
    east = jnp.where(
        lane == width - 1,
        pltpu.roll(right, width - 1 - i, axis=1),
        pltpu.roll(here, width - 1, axis=1),
    )
    return (
        weights[0] * here
        + weights[1] * rows[i]
        + weights[2] * rows[i + 2]
        + weights[3] * west
        + weights[4] * east
    )


def keep_edges(edge_ref, row, i, count):
    feat, width = row.shape
    lane = lax.broadcasted_iota(jnp.int32, (feat, width), 1)
    edge_ref[...] = jnp.where(
        lane == i,
        pltpu.roll(row, i, axis=1),
        jnp.where(
            lane == count + i,
            pltpu.roll(row, lax.rem(count + i + 1, width), axis=1),
            edge_ref[...],
        ),
    )


def weights_of(c_ref, order, width):
    feat = c_ref.shape[0]
    return [jnp.broadcast_to(c_ref[:, k : k + 1], (feat, width)) for k in order]


def mm(a, b):
    return jnp.dot(a, b, preferred_element_type=jnp.float32)


def mm_nt(a, b):
    return lax.dot_general(a, b, (((1,), (1,)), ((), ())), preferred_element_type=jnp.float32)


def two_parts(x):
    high = x.astype(jnp.bfloat16)
    low = (x - high.astype(jnp.float32)).astype(jnp.bfloat16)
    return jnp.concatenate([high, low], axis=0)


def forward_group(rows, left, right, weights, wit_ref, wot_ref, base):
    width = rows.shape[2]
    inputs = jnp.concatenate([rows[base + g + 1] for g in range(GROUP)], axis=1).astype(
        jnp.bfloat16
    )
    hidden = jnp.tanh(mm(wit_ref[...], inputs)).astype(jnp.bfloat16)
    closure = mm(wot_ref[...], hidden)
    return [
        stencil_row(rows, left, right, weights, base + g) + closure[:, g * width : (g + 1) * width]
        for g in range(GROUP)
    ]


def forward_kernel(
    x_ref, n_ref, s_ref, l_ref, r_ref, c_ref, wit_ref, wot_ref, o_ref, edge_ref, rows
):
    count, feat, width = x_ref.shape
    fill_rows(rows, x_ref, n_ref, s_ref)
    edge_ref[...] = jnp.zeros_like(edge_ref)

    def step(b, carry):
        base = b * GROUP
        weights = weights_of(c_ref, (0, 1, 2, 3, 4), width)
        out = forward_group(
            rows, l_ref[...], r_ref[...], weights, wit_ref, wot_ref, base
        )
        for g in range(GROUP):
            o_ref[base + g] = out[g]
            keep_edges(edge_ref, out[g], base + g, count)
        return carry

    lax.fori_loop(0, count // GROUP, step, 0)


def forward_interp_kernel(
    x_ref, n_ref, s_ref, l_ref, r_ref, c_ref, wit_ref, wot_ref, cell_ref, o_ref, rows, acc
):
    count, feat, width = x_ref.shape
    slots = cell_ref.shape[1]
    block = min(slots, 512)
    fill_rows(rows, x_ref, n_ref, s_ref)
    acc[...] = jnp.zeros_like(acc)

    def step(b, carry):
        base = b * GROUP
        weights = weights_of(c_ref, (0, 1, 2, 3, 4), width)
        out = forward_group(
            rows, l_ref[...], r_ref[...], weights, wit_ref, wot_ref, base
        )
        parts = two_parts(jnp.concatenate(out, axis=1))
        for s in range(0, slots, block):
            cell = (
                lax.broadcasted_iota(jnp.int32, (GROUP * width, block), 0) + base * width
            )
            pick = jnp.zeros((GROUP * width, block), jnp.float32)
            for k in range(4):
                pick = pick + jnp.where(
                    cell == cell_ref[k : k + 1, s : s + block], float(corner_tenths[k]), 0.0
                )
            both = mm(parts, pick.astype(jnp.bfloat16))
            acc[:, s : s + block] += both[:feat] + both[feat:]
        return carry

    lax.fori_loop(0, count // GROUP, step, 0)
    blocks = jnp.transpose(acc[...] * TENTH).reshape(slots // CAP, CAP, feat)
    o_ref[...] = jnp.concatenate([blocks[:, : CAP // 2], blocks[:, CAP // 2 :]], axis=2)


def spread_kernel(pulled_ref, cell_ref, o_ref, edge_ref, parts):
    count, feat, width = o_ref.shape
    slots = cell_ref.shape[0]
    edge_ref[...] = jnp.zeros_like(edge_ref)
    blocks = pulled_ref[...]
    pulled = jnp.concatenate([blocks[:, :, :feat], blocks[:, :, feat:]], axis=1)
    parts[...] = two_parts(jnp.transpose(pulled.reshape(slots, feat)) * TENTH)
    block = min(slots, 512)

    def step(b, carry):
        base = b * GROUP
        total = jnp.zeros((2 * feat, GROUP * width), jnp.float32)
        for s in range(0, slots, block):
            cell = (
                lax.broadcasted_iota(jnp.int32, (block, GROUP * width), 1) + base * width
            )
            pick = jnp.zeros((block, GROUP * width), jnp.float32)
            for k in range(4):
                pick = pick + jnp.where(
                    cell == cell_ref[s : s + block, k : k + 1], float(corner_tenths[k]), 0.0
                )
            total = total + mm(parts[:, s : s + block], pick.astype(jnp.bfloat16))
        out = total[:feat] + total[feat:]
        for g in range(GROUP):
            row = out[:, g * width : (g + 1) * width]
            o_ref[base + g] = row
            keep_edges(edge_ref, row, base + g, count)
        return carry

    lax.fori_loop(0, count // GROUP, step, 0)


def backward_kernel(
    v_ref,
    x_ref,
    n_ref,
    s_ref,
    l_ref,
    r_ref,
    c_ref,
    wit_ref,
    wi_ref,
    wo_ref,
    o_ref,
    edge_ref,
    grad_ref,
    rows,
    gin,
    gout,
):
    count, feat, width = x_ref.shape
    fill_rows(rows, x_ref, n_ref, s_ref)
    edge_ref[...] = jnp.zeros_like(edge_ref)
    gin[...] = jnp.zeros_like(gin)
    gout[...] = jnp.zeros_like(gout)

    def step(b, carry):
        base = b * GROUP
        weights = weights_of(c_ref, (0, 2, 1, 4, 3), width)
        inputs = jnp.concatenate([v_ref[base + g] for g in range(GROUP)], axis=1).astype(
            jnp.bfloat16
        )
        cot = jnp.concatenate([rows[base + g + 1] for g in range(GROUP)], axis=1).astype(
            jnp.bfloat16
        )
        tanh_pre = jnp.tanh(mm(wit_ref[...], inputs))
        hidden = tanh_pre.astype(jnp.bfloat16)
        gout[...] += mm_nt(hidden, cot)
        back_hidden = mm(wo_ref[...], cot)
        back_pre = (back_hidden * (1.0 - tanh_pre * tanh_pre)).astype(jnp.bfloat16)
        gin[...] += mm_nt(back_pre, inputs)
        back = mm(wi_ref[...], back_pre)
        for g in range(GROUP):
            row = (
                stencil_row(rows, l_ref[...], r_ref[...], weights, base + g)
                + back[:, g * width : (g + 1) * width]
            )
            o_ref[base + g] = row
            keep_edges(edge_ref, row, base + g, count)
        return carry

    lax.fori_loop(0, count // GROUP, step, 0)
    grad_ref[...] = jnp.concatenate([gin[...], gout[...]], axis=1)


def call(kernel, outs, scratch, *args):
    return pl.pallas_call(
        kernel,
        out_shape=outs,
        in_specs=[pl.BlockSpec(memory_space=pltpu.VMEM)] * len(args),
        out_specs=jax.tree.map(lambda _: pl.BlockSpec(memory_space=pltpu.VMEM), outs),
        scratch_shapes=scratch,
        compiler_params=pltpu.CompilerParams(vmem_limit_bytes=VMEM_LIMIT),
    )(*args)


def place(index):
    lon = lax.axis_size("lon")
    return {"lat": index // lon, "lon": lax.rem(index, lon)}


def remote(src, dst, send, recv, to):
    return pltpu.make_async_remote_copy(
        src_ref=src,
        dst_ref=dst,
        send_sem=send,
        recv_sem=recv,
        device_id=to,
        device_id_type=pl.DeviceIdType.MESH,
    )


def signal(sem, to):
    pl.semaphore_signal(sem, inc=1, device_id=to, device_id_type=pl.DeviceIdType.MESH)


def exchange_kernel(mode, halo, *refs):
    refs = list(refs)
    take = lambda k: [refs.pop(0) for _ in range(k)]
    field, edges = take(2) if halo else (None, None)
    (blocks,) = take(1) if mode else (None,)
    halo_out = take(4) if halo else ()
    (blocks_out,) = take(1) if mode else (None,)
    halo_send, halo_recv = take(2) if halo else (None, None)
    send, recv, own_sem = take(3) if mode else (None, None, None)

    lat, lon = lax.axis_index("lat"), lax.axis_index("lon")
    lats, lons = lax.axis_size("lat"), lax.axis_size("lon")
    devices = lats * lons
    me = lat * lons + lon
    south, north = {"lat": lax.rem(lat + 1, lats)}, {"lat": lax.rem(lat + lats - 1, lats)}
    east, west = {"lon": lax.rem(lon + 1, lons)}, {"lon": lax.rem(lon + lons - 1, lons)}

    barrier = pltpu.get_barrier_semaphore()
    if mode:

        def greet(k, carry):
            signal(barrier, place(lax.rem(me + k, devices)))
            return carry

        lax.fori_loop(1, devices, greet, 0)
        pl.semaphore_wait(barrier, devices - 1)
    else:
        for to in (south, north, east, west):
            signal(barrier, to)
        pl.semaphore_wait(barrier, 4)

    halo_copies = []
    if halo:
        count = field.shape[0]
        sources = (field.at[count - 1], field.at[0], edges, edges)
        for k, to in enumerate((south, north, east, west)):
            halo_copies.append(
                remote(sources[k], halo_out[k], halo_send.at[k], halo_recv.at[k], to)
            )
            halo_copies[-1].start()
    if mode:

        def copy_to(k):
            peer = lax.rem(me + k, devices)
            source = blocks.at[peer] if mode == "swap" else blocks
            return remote(source, blocks_out.at[me], send.at[k], recv.at[k], place(peer))

        def start(k, carry):
            copy_to(k).start()
            return carry

        def finish(k, carry):
            copy_to(k).wait()
            return carry

        lax.fori_loop(1, devices, start, 0)
        own = pltpu.make_async_copy(
            blocks.at[me] if mode == "swap" else blocks, blocks_out.at[me], own_sem.at[0]
        )
        own.start()
        own.wait()
        lax.fori_loop(1, devices, finish, 0)
    for copy in halo_copies:
        copy.wait()
    if halo:

        @pl.when(lat == 0)
        def _():
            halo_out[0][...] = jnp.zeros_like(halo_out[0])

        @pl.when(lat == lats - 1)
        def _():
            halo_out[1][...] = jnp.zeros_like(halo_out[1])


def exchange(number, mode=None, blocks=None, field=None, edges=None):
    devices = lax.axis_size("lat") * lax.axis_size("lon")
    halo = field is not None
    vmem, dma = pl.BlockSpec(memory_space=pltpu.VMEM), pltpu.SemaphoreType.DMA
    args, specs, outs, scratch = [], [], [], []
    if halo:
        args += [field, edges]
        specs += [pl.BlockSpec(memory_space=pl.ANY), vmem]
        outs += [jax.ShapeDtypeStruct(edges.shape, edges.dtype)] * 4
        scratch += [dma((4,)), dma((4,))]
    if mode:
        block = blocks.shape[1:] if mode == "swap" else blocks.shape
        args.append(blocks)
        specs.append(vmem)
        outs.append(jax.ShapeDtypeStruct((devices,) + block, blocks.dtype))
        scratch += [dma((devices,)), dma((devices,)), dma((1,))]
    return pl.pallas_call(
        functools.partial(exchange_kernel, mode, halo),
        out_shape=outs,
        in_specs=specs,
        out_specs=[vmem] * len(outs),
        scratch_shapes=scratch,
        compiler_params=pltpu.CompilerParams(
            collective_id=number, has_side_effects=True, vmem_limit_bytes=16 * 1024 * 1024
        ),
    )(*args)


def edge_kernel(x_ref, edge_ref):
    count = x_ref.shape[0]
    edge_ref[...] = jnp.zeros_like(edge_ref)

    def step(i, carry):
        keep_edges(edge_ref, x_ref[i], i, count)
        return carry

    lax.fori_loop(0, count, step, 0, unroll=4)


def f32(*shape):
    return jax.ShapeDtypeStruct(shape, jnp.float32)


def on_device(
    start_state, coefficients, w_in, w_out, jacobian, sigma, obs_values, owner, stencil, counts
):
    tlat, feat, tlon = start_state.shape
    hid = w_in.shape[1]
    lat_count = lax.axis_size("lat")
    lon_count = lax.axis_size("lon")
    devices = lat_count * lon_count
    channels = obs_values.shape[1]
    slots = devices * CAP
    rows_scratch = pltpu.VMEM((tlat + 2, feat, tlon), jnp.float32)
    tile, edge_shape = f32(tlat, feat, tlon), f32(feat, tlon)

    tile_owner = owner[:, 0]
    onehot = (tile_owner[:, None] == jnp.arange(devices, dtype=jnp.int32)[None, :]).astype(
        jnp.int32
    )
    running = jnp.cumsum(onehot, axis=0)
    rank = jnp.sum(running * onehot, axis=1) - 1
    slot = tile_owner * CAP + rank
    send_stencil = jnp.zeros((slots, 4), jnp.int32).at[slot].set(stencil)

    coef = coefficients.T
    w_in_t, w_out_t = w_in.T, w_out.T
    start_edges = call(edge_kernel, edge_shape, [], start_state)
    state_one, edges_one = call(
        forward_kernel,
        (tile, edge_shape),
        [rows_scratch],
        start_state,
        *exchange(0, field=start_state, edges=start_edges),
        coef,
        w_in_t,
        w_out_t,
    )
    *halo_one, cell_recv = exchange(
        1,
        "swap",
        send_stencil.reshape(devices, 1, CAP * 4),
        field=state_one,
        edges=edges_one,
    )
    cell_recv = cell_recv.reshape(slots, 4)
    slot_interp = call(
        forward_interp_kernel,
        f32(devices, CAP // 2, 2 * feat),
        [rows_scratch, pltpu.VMEM((feat, slots), jnp.float32)],
        state_one,
        *halo_one,
        coef,
        w_in_t,
        w_out_t,
        cell_recv.T,
    )
    half = (rank >= CAP // 2)[:, None]
    packed = tile_owner * (CAP // 2) + rank % (CAP // 2)
    (interp,) = exchange(2, "swap", slot_interp)
    both = interp.reshape(slots // 2, 2 * feat)[packed]
    row_interp = jnp.where(half, both[:, feat:], both[:, :feat])
    evolved = jnp.dot(
        row_interp, jacobian.T, precision=lax.Precision.HIGHEST, preferred_element_type=jnp.float32
    )
    used = jnp.arange(channels, dtype=jnp.int32)[None, :] < counts[:, None]
    departures = jnp.where(used, (obs_values - evolved) / sigma[None, :], 0.0)
    row_pulled = jnp.dot(
        -departures / sigma[None, :],
        jacobian,
        precision=lax.Precision.HIGHEST,
        preferred_element_type=jnp.float32,
    )
    row_pair = jnp.concatenate(
        [jnp.where(half, 0.0, row_pulled), jnp.where(half, row_pulled, 0.0)], axis=1
    )
    send_pulled = jnp.zeros((slots // 2, 2 * feat), jnp.float32).at[packed].add(row_pair)
    (recv_pulled,) = exchange(
        3, "swap", send_pulled.reshape(devices, CAP // 2, 2 * feat)
    )
    adjoint_two, edges_two = call(
        spread_kernel,
        (tile, edge_shape),
        [pltpu.VMEM((2 * feat, slots), jnp.bfloat16)],
        recv_pulled,
        cell_recv,
    )

    def backward(number, state, cotangent, edges):
        return call(
            backward_kernel,
            (tile, edge_shape, f32(hid, 2 * feat)),
            [rows_scratch] + [pltpu.VMEM((hid, feat), jnp.float32)] * 2,
            state,
            cotangent,
            *exchange(number, field=cotangent, edges=edges),
            coef,
            w_in_t,
            w_in,
            w_out,
        )

    adjoint_one, edges_adj, grads_one = backward(4, state_one, adjoint_two, edges_two)
    grad_state, _, grads_zero = backward(5, start_state, adjoint_one, edges_adj)
    grads = (grads_one + grads_zero).reshape(devices, hid // devices, 2 * feat)
    part = jnp.sum(exchange(6, "swap", grads)[0], axis=0)
    scale = 1.0 / math.sqrt(tlat * lat_count * tlon * lon_count)
    total = exchange(7, "spread", part * scale)[0].reshape(hid, 2 * feat)
    return (grad_state, departures, total[:, :feat].T, total[:, feat:])


def solution(mesh):
    return jax.shard_map(
        on_device,
        mesh=mesh,
        in_specs=(
            P("lat", None, "lon"),
            P(),
            P(),
            P(),
            P(),
            P(),
            P(("lat", "lon"), None),
            P(("lat", "lon"), None),
            P(("lat", "lon"), None),
            P(("lat", "lon")),
        ),
        out_specs=(P("lat", None, "lon"), P(("lat", "lon"), None), P(), P()),
        check_vma=False,
    )
```

```python
import functools
import math

import jax
import jax.numpy as jnp
from jax import lax
from jax.experimental import pallas as pl
from jax.experimental.pallas import tpu as pltpu
from jax.sharding import PartitionSpec as P

CAP = 16
GROUP = 4
BACK_GROUP = 8
VMEM_LIMIT = 48 * 1024 * 1024
corner_tenths = (4, 3, 2, 1)
TENTH = 0.1


def fill_rows(rows, x_ref, north_ref, south_ref):
    count = x_ref.shape[0]
    rows[pl.ds(1, count)] = x_ref[...]
    rows[0] = north_ref[...]
    rows[count + 1] = south_ref[...]


def stencil_row(rows, left, right, weights, i):
    count, (feat, width) = rows.shape[0] - 2, rows.shape[1:]
    lane = lax.broadcasted_iota(jnp.int32, (feat, width), 1)
    here = rows[i + 1]
    west = jnp.where(
        lane == 0, pltpu.roll(left, width - count - i, axis=1), pltpu.roll(here, 1, axis=1)
    )
    east = jnp.where(
        lane == width - 1,
        pltpu.roll(right, width - 1 - i, axis=1),
        pltpu.roll(here, width - 1, axis=1),
    )
    return (
        weights[0] * here
        + weights[1] * rows[i]
        + weights[2] * rows[i + 2]
        + weights[3] * west
        + weights[4] * east
    )


def keep_edges(edge_ref, row, i, count):
    feat, width = row.shape
    lane = lax.broadcasted_iota(jnp.int32, (feat, width), 1)
    edge_ref[...] = jnp.where(
        lane == i,
        pltpu.roll(row, i, axis=1),
        jnp.where(
            lane == count + i,
            pltpu.roll(row, lax.rem(count + i + 1, width), axis=1),
            edge_ref[...],
        ),
    )


def weights_of(c_ref, order, width):
    feat = c_ref.shape[0]
    return [jnp.broadcast_to(c_ref[:, k : k + 1], (feat, width)) for k in order]


def mm(a, b):
    return jnp.dot(a, b, preferred_element_type=jnp.float32)


def mm_nt(a, b):
    return lax.dot_general(a, b, (((1,), (1,)), ((), ())), preferred_element_type=jnp.float32)


def two_parts(x):
    high = x.astype(jnp.bfloat16)
    low = (x - high.astype(jnp.float32)).astype(jnp.bfloat16)
    return jnp.concatenate([high, low], axis=0)


def picks(local, cells):
    slots = local.shape[1]
    low = local.astype(jnp.int16)
    cell = lax.broadcasted_iota(jnp.int16, (cells, slots), 0)
    zero = jnp.zeros((cells, slots), jnp.bfloat16)
    pick = zero
    for k in range(4):
        same = cell == jnp.broadcast_to(low[k : k + 1], (cells, slots))
        pick = pick + jnp.where(same, jnp.full_like(zero, corner_tenths[k]), zero)
    return pick


def forward_group(rows, left, right, weights, wit_ref, wot_ref, base):
    width = rows.shape[2]
    inputs = jnp.concatenate([rows[base + g + 1] for g in range(GROUP)], axis=1).astype(
        jnp.bfloat16
    )
    hidden = jnp.tanh(mm(wit_ref[...], inputs)).astype(jnp.bfloat16)
    closure = mm(wot_ref[...], hidden)
    return [
        stencil_row(rows, left, right, weights, base + g) + closure[:, g * width : (g + 1) * width]
        for g in range(GROUP)
    ]


def forward_kernel(
    x_ref, n_ref, s_ref, l_ref, r_ref, c_ref, wit_ref, wot_ref, o_ref, edge_ref, rows
):
    count, feat, width = x_ref.shape
    fill_rows(rows, x_ref, n_ref, s_ref)
    edge_ref[...] = jnp.zeros_like(edge_ref)

    def step(b, carry):
        base = b * GROUP
        weights = weights_of(c_ref, (0, 1, 2, 3, 4), width)
        out = forward_group(
            rows, l_ref[...], r_ref[...], weights, wit_ref, wot_ref, base
        )
        for g in range(GROUP):
            o_ref[base + g] = out[g]
            keep_edges(edge_ref, out[g], base + g, count)
        return carry

    lax.fori_loop(0, count // GROUP, step, 0)


def forward_interp_kernel(
    x_ref, n_ref, s_ref, l_ref, r_ref, c_ref, wit_ref, wot_ref, cell_ref, o_ref, rows, acc
):
    count, feat, width = x_ref.shape
    slots = cell_ref.shape[1]
    block = min(slots, 512)
    fill_rows(rows, x_ref, n_ref, s_ref)
    acc[...] = jnp.zeros_like(acc)

    def step(b, carry):
        base = b * GROUP
        weights = weights_of(c_ref, (0, 1, 2, 3, 4), width)
        out = forward_group(
            rows, l_ref[...], r_ref[...], weights, wit_ref, wot_ref, base
        )
        parts = two_parts(jnp.concatenate(out, axis=1))
        for s in range(0, slots, block):
            both = mm(parts, picks(cell_ref[:, s : s + block] - base * width, GROUP * width))
            acc[:, s : s + block] += both[:feat] + both[feat:]
        return carry

    lax.fori_loop(0, count // GROUP, step, 0)
    blocks = jnp.transpose(acc[...] * TENTH).reshape(slots // CAP, CAP, feat)
    o_ref[...] = jnp.concatenate([blocks[:, : CAP // 2], blocks[:, CAP // 2 :]], axis=2)


def spread_kernel(pulled_ref, cell_ref, o_ref, edge_ref, parts):
    count, feat, width = o_ref.shape
    slots = cell_ref.shape[1]
    edge_ref[...] = jnp.zeros_like(edge_ref)
    blocks = pulled_ref[...]
    pulled = jnp.concatenate([blocks[:, :, :feat], blocks[:, :, feat:]], axis=1)
    parts[...] = two_parts(jnp.transpose(pulled.reshape(slots, feat)) * TENTH)
    block = min(slots, 512)

    def step(b, carry):
        base = b * GROUP
        total = jnp.zeros((2 * feat, GROUP * width), jnp.float32)
        for s in range(0, slots, block):
            pick = picks(cell_ref[:, s : s + block] - base * width, GROUP * width)
            total = total + mm_nt(parts[:, s : s + block], pick)
        out = total[:feat] + total[feat:]
        for g in range(GROUP):
            row = out[:, g * width : (g + 1) * width]
            o_ref[base + g] = row
            keep_edges(edge_ref, row, base + g, count)
        return carry

    lax.fori_loop(0, count // GROUP, step, 0)


def backward_kernel(
    v_ref,
    x_ref,
    n_ref,
    s_ref,
    l_ref,
    r_ref,
    c_ref,
    wit_ref,
    wi_ref,
    wo_ref,
    o_ref,
    edge_ref,
    grad_ref,
    rows,
    gin,
    gout,
):
    count, feat, width = x_ref.shape
    fill_rows(rows, x_ref, n_ref, s_ref)
    edge_ref[...] = jnp.zeros_like(edge_ref)
    gin[...] = jnp.zeros_like(gin)
    gout[...] = jnp.zeros_like(gout)

    def step(b, carry):
        base = b * BACK_GROUP
        weights = weights_of(c_ref, (0, 2, 1, 4, 3), width)
        inputs = jnp.concatenate([v_ref[base + g] for g in range(BACK_GROUP)], axis=1).astype(
            jnp.bfloat16
        )
        cot = jnp.concatenate([rows[base + g + 1] for g in range(BACK_GROUP)], axis=1).astype(
            jnp.bfloat16
        )
        tanh_pre = jnp.tanh(mm(wit_ref[...], inputs))
        hidden = tanh_pre.astype(jnp.bfloat16)
        gout[...] += mm_nt(hidden, cot)
        back_hidden = mm(wo_ref[...], cot)
        back_pre = (back_hidden * (1.0 - tanh_pre * tanh_pre)).astype(jnp.bfloat16)
        gin[...] += mm_nt(back_pre, inputs)
        back = mm(wi_ref[...], back_pre)
        for g in range(BACK_GROUP):
            row = (
                stencil_row(rows, l_ref[...], r_ref[...], weights, base + g)
                + back[:, g * width : (g + 1) * width]
            )
            o_ref[base + g] = row
            keep_edges(edge_ref, row, base + g, count)
        return carry

    lax.fori_loop(0, count // BACK_GROUP, step, 0)
    grad_ref[...] = jnp.concatenate([gin[...], gout[...]], axis=1)


def call(kernel, outs, scratch, *args):
    return pl.pallas_call(
        kernel,
        out_shape=outs,
        in_specs=[pl.BlockSpec(memory_space=pltpu.VMEM)] * len(args),
        out_specs=jax.tree.map(lambda _: pl.BlockSpec(memory_space=pltpu.VMEM), outs),
        scratch_shapes=scratch,
        compiler_params=pltpu.CompilerParams(vmem_limit_bytes=VMEM_LIMIT),
    )(*args)


def place(index):
    lon = lax.axis_size("lon")
    return {"lat": index // lon, "lon": lax.rem(index, lon)}


def remote(src, dst, send, recv, to):
    return pltpu.make_async_remote_copy(
        src_ref=src,
        dst_ref=dst,
        send_sem=send,
        recv_sem=recv,
        device_id=to,
        device_id_type=pl.DeviceIdType.MESH,
    )


def signal(sem, to):
    pl.semaphore_signal(sem, inc=1, device_id=to, device_id_type=pl.DeviceIdType.MESH)


def exchange_kernel(mode, halo, *refs):
    refs = list(refs)
    take = lambda k: [refs.pop(0) for _ in range(k)]
    field, edges = take(2) if halo else (None, None)
    (blocks,) = take(1) if mode else (None,)
    halo_out = take(4) if halo else ()
    (blocks_out,) = take(1) if mode else (None,)
    halo_send, halo_recv = take(2) if halo else (None, None)
    send, recv, own_sem = take(3) if mode else (None, None, None)

    lat, lon = lax.axis_index("lat"), lax.axis_index("lon")
    lats, lons = lax.axis_size("lat"), lax.axis_size("lon")
    devices = lats * lons
    me = lat * lons + lon
    south, north = {"lat": lax.rem(lat + 1, lats)}, {"lat": lax.rem(lat + lats - 1, lats)}
    east, west = {"lon": lax.rem(lon + 1, lons)}, {"lon": lax.rem(lon + lons - 1, lons)}

    barrier = pltpu.get_barrier_semaphore()
    if mode:

        def greet(k, carry):
            signal(barrier, place(lax.rem(me + k, devices)))
            return carry

        lax.fori_loop(1, devices, greet, 0)
        pl.semaphore_wait(barrier, devices - 1)
    else:
        for to in (south, north, east, west):
            signal(barrier, to)
        pl.semaphore_wait(barrier, 4)

    halo_copies = []
    if halo:
        count = field.shape[0]
        sources = (field.at[count - 1], field.at[0], edges, edges)
        for k, to in enumerate((south, north, east, west)):
            halo_copies.append(
                remote(sources[k], halo_out[k], halo_send.at[k], halo_recv.at[k], to)
            )
            halo_copies[-1].start()
    if mode:

        def copy_to(k):
            peer = lax.rem(me + k, devices)
            source = blocks.at[peer] if mode == "swap" else blocks
            return remote(source, blocks_out.at[me], send.at[k], recv.at[k], place(peer))

        def start(k, carry):
            copy_to(k).start()
            return carry

        def finish(k, carry):
            copy_to(k).wait()
            return carry

        lax.fori_loop(1, devices, start, 0)
        own = pltpu.make_async_copy(
            blocks.at[me] if mode == "swap" else blocks, blocks_out.at[me], own_sem.at[0]
        )
        own.start()
        own.wait()
        lax.fori_loop(1, devices, finish, 0)
    for copy in halo_copies:
        copy.wait()
    if halo:

        @pl.when(lat == 0)
        def _():
            halo_out[0][...] = jnp.zeros_like(halo_out[0])

        @pl.when(lat == lats - 1)
        def _():
            halo_out[1][...] = jnp.zeros_like(halo_out[1])


def exchange(number, mode=None, blocks=None, field=None, edges=None):
    devices = lax.axis_size("lat") * lax.axis_size("lon")
    halo = field is not None
    vmem, dma = pl.BlockSpec(memory_space=pltpu.VMEM), pltpu.SemaphoreType.DMA
    args, specs, outs, scratch = [], [], [], []
    if halo:
        args += [field, edges]
        specs += [pl.BlockSpec(memory_space=pl.ANY), vmem]
        outs += [jax.ShapeDtypeStruct(edges.shape, edges.dtype)] * 4
        scratch += [dma((4,)), dma((4,))]
    if mode:
        block = blocks.shape[1:] if mode == "swap" else blocks.shape
        args.append(blocks)
        specs.append(vmem)
        outs.append(jax.ShapeDtypeStruct((devices,) + block, blocks.dtype))
        scratch += [dma((devices,)), dma((devices,)), dma((1,))]
    return pl.pallas_call(
        functools.partial(exchange_kernel, mode, halo),
        out_shape=outs,
        in_specs=specs,
        out_specs=[vmem] * len(outs),
        scratch_shapes=scratch,
        compiler_params=pltpu.CompilerParams(
            collective_id=number, has_side_effects=True, vmem_limit_bytes=16 * 1024 * 1024
        ),
    )(*args)


def edge_kernel(x_ref, edge_ref):
    count = x_ref.shape[0]
    edge_ref[...] = jnp.zeros_like(edge_ref)

    def step(i, carry):
        keep_edges(edge_ref, x_ref[i], i, count)
        return carry

    lax.fori_loop(0, count, step, 0, unroll=4)


def f32(*shape):
    return jax.ShapeDtypeStruct(shape, jnp.float32)


def on_device(
    start_state, coefficients, w_in, w_out, jacobian, sigma, obs_values, owner, stencil, counts
):
    tlat, feat, tlon = start_state.shape
    assert tlat * tlon <= 1 << 15
    hid = w_in.shape[1]
    lat_count = lax.axis_size("lat")
    lon_count = lax.axis_size("lon")
    devices = lat_count * lon_count
    channels = obs_values.shape[1]
    slots = devices * CAP
    rows_scratch = pltpu.VMEM((tlat + 2, feat, tlon), jnp.float32)
    tile, edge_shape = f32(tlat, feat, tlon), f32(feat, tlon)

    tile_owner = owner[:, 0]
    onehot = (tile_owner[:, None] == jnp.arange(devices, dtype=jnp.int32)[None, :]).astype(
        jnp.int32
    )
    running = jnp.cumsum(onehot, axis=0)
    rank = jnp.sum(running * onehot, axis=1) - 1
    slot = tile_owner * CAP + rank
    send_stencil = jnp.zeros((slots, 4), jnp.int32).at[slot].set(stencil)

    coef = coefficients.T
    w_in_t, w_out_t = w_in.T, w_out.T
    start_edges = call(edge_kernel, edge_shape, [], start_state)
    state_one, edges_one = call(
        forward_kernel,
        (tile, edge_shape),
        [rows_scratch],
        start_state,
        *exchange(0, field=start_state, edges=start_edges),
        coef,
        w_in_t,
        w_out_t,
    )
    *halo_one, cell_recv = exchange(
        1,
        "swap",
        send_stencil.reshape(devices, 1, CAP * 4),
        field=state_one,
        edges=edges_one,
    )
    cell_recv = cell_recv.reshape(slots, 4)
    slot_interp = call(
        forward_interp_kernel,
        f32(devices, CAP // 2, 2 * feat),
        [rows_scratch, pltpu.VMEM((feat, slots), jnp.float32)],
        state_one,
        *halo_one,
        coef,
        w_in_t,
        w_out_t,
        cell_recv.T,
    )
    half = (rank >= CAP // 2)[:, None]
    packed = tile_owner * (CAP // 2) + rank % (CAP // 2)
    (interp,) = exchange(2, "swap", slot_interp)
    both = interp.reshape(slots // 2, 2 * feat)[packed]
    row_interp = jnp.where(half, both[:, feat:], both[:, :feat])
    evolved = jnp.dot(
        row_interp, jacobian.T, precision=lax.Precision.HIGHEST, preferred_element_type=jnp.float32
    )
    used = jnp.arange(channels, dtype=jnp.int32)[None, :] < counts[:, None]
    departures = jnp.where(used, (obs_values - evolved) / sigma[None, :], 0.0)
    row_pulled = jnp.dot(
        -departures / sigma[None, :],
        jacobian,
        precision=lax.Precision.HIGHEST,
        preferred_element_type=jnp.float32,
    )
    row_pair = jnp.concatenate(
        [jnp.where(half, 0.0, row_pulled), jnp.where(half, row_pulled, 0.0)], axis=1
    )
    send_pulled = jnp.zeros((slots // 2, 2 * feat), jnp.float32).at[packed].add(row_pair)
    (recv_pulled,) = exchange(
        3, "swap", send_pulled.reshape(devices, CAP // 2, 2 * feat)
    )
    adjoint_two, edges_two = call(
        spread_kernel,
        (tile, edge_shape),
        [pltpu.VMEM((2 * feat, slots), jnp.bfloat16)],
        recv_pulled,
        cell_recv.T,
    )

    def backward(number, state, cotangent, edges):
        return call(
            backward_kernel,
            (tile, edge_shape, f32(hid, 2 * feat)),
            [rows_scratch] + [pltpu.VMEM((hid, feat), jnp.float32)] * 2,
            state,
            cotangent,
            *exchange(number, field=cotangent, edges=edges),
            coef,
            w_in_t,
            w_in,
            w_out,
        )

    adjoint_one, edges_adj, grads_one = backward(4, state_one, adjoint_two, edges_two)
    grad_state, _, grads_zero = backward(5, start_state, adjoint_one, edges_adj)
    grads = (grads_one + grads_zero).reshape(devices, hid // devices, 2 * feat)
    part = jnp.sum(exchange(6, "swap", grads)[0], axis=0)
    scale = 1.0 / math.sqrt(tlat * lat_count * tlon * lon_count)
    total = exchange(7, "spread", part * scale)[0].reshape(hid, 2 * feat)
    return (grad_state, departures, total[:, :feat].T, total[:, feat:])


def solution(mesh):
    return jax.shard_map(
        on_device,
        mesh=mesh,
        in_specs=(
            P("lat", None, "lon"),
            P(),
            P(),
            P(),
            P(),
            P(),
            P(("lat", "lon"), None),
            P(("lat", "lon"), None),
            P(("lat", "lon"), None),
            P(("lat", "lon")),
        ),
        out_specs=(P("lat", None, "lon"), P(("lat", "lon"), None), P(), P()),
        check_vma=False,
    )
```
